512 devices in a mesh: fr: 4 (over z_lo), py: 8 (over x, core), px: 16 (over z_hi, y).
Axes of the slice: x: 4, y: 4, z: 16 (z_hi: 4, z_lo: 4; z = z_hi * 4 + z_lo), core: 2. Of those that a mesh axis runs over, the one named last changes fastest.
Arguments:
- recording: bfloat16 [640, 512, 2048], P('fr', 'py', 'px'), may hold values from -9 to 9
- shifts: int32 [640, 2], P('fr'), may hold values from -32 to 32, as said below
- components: bfloat16 [640, 256], P('fr'), may hold values from -0.3125 to 0.3125
Outputs:
- projection: bfloat16 [256, 512, 2048], P('fr', 'py', 'px')
The draws below stay inside these ranges and needn't reach their ends.
Inputs may be any that keep to these rules, and one draw needn't show every extreme that they name: `shifts`: some frame has row shift 32 and some frame has column shift -32.
All inputs are finite; a program needn't handle non-finite values.
Results may differ from the reference program's by a relative error of at most 0.014.
Values may be sent and summed in bfloat16 or wider, within the bound.
A program may use at most 64 MiB of HBM per device.

```python
import math
import jax
import jax.numpy as jnp
from jax import lax

FRAMES_DEV = 160
TILE_ROWS = 64
COMPONENT_COUNT = 256
SHIFT_MAX = 32
RADIUS = 4
FRAMES = 640
HEIGHT = 512
WIDTH = 2048
N_FR = 4
N_PY = 8


def draw_recording(key, part):
    keys = jax.random.split(key, 5)
    shape = (FRAMES, HEIGHT, WIDTH)
    rows = lax.broadcasted_iota(jnp.float32, shape, 1)
    columns = lax.broadcasted_iota(jnp.float32, shape, 2)
    period = 16.0 * RADIUS
    row_phase = jax.random.uniform(keys[3], (FRAMES, HEIGHT, 1), jnp.float32, -math.pi, math.pi)
    col_phase = jax.random.uniform(keys[4], (FRAMES, 1, WIDTH), jnp.float32, -math.pi, math.pi)
    noise = 0.5 * jax.random.truncated_normal(keys[0], -4.0, 4.0, shape, jnp.float32)
    row_amp = 1.4 * jax.random.truncated_normal(keys[1], -2.5, 2.5, (FRAMES, HEIGHT, 1), jnp.float32)
    col_amp = 1.4 * jax.random.truncated_normal(keys[2], -2.5, 2.5, (FRAMES, 1, WIDTH), jnp.float32)
    stripes = row_amp * jnp.cos(2.0 * math.pi * columns / period + row_phase) + col_amp * jnp.cos(2.0 * math.pi * rows / period + col_phase)
    return (noise + stripes).astype(jnp.bfloat16)


def draw_shifts(key, part):
    keys = jax.random.split(key, 3)
    base = jax.random.randint(keys[0], (FRAMES, 2), -SHIFT_MAX, SHIFT_MAX + 1, jnp.int32)
    first_frame = jax.random.randint(keys[1], (), 0, FRAMES, jnp.int32)
    second_frame = jax.random.randint(keys[2], (), 0, FRAMES, jnp.int32)
    base = base.at[first_frame, 0].set(SHIFT_MAX)
    base = base.at[second_frame, 1].set(-SHIFT_MAX)
    return base


def strengthened(values, rng, source, target, shards_of, factor):
    def block_of(axis_at):
        return (jnp.arange(values.shape[axis_at]) // (values.shape[axis_at] // shards_of)).reshape((-1,) + (1,) * (values.ndim - 1 - axis_at))

    first = jax.random.permutation(rng, shards_of)[block_of(target)]
    far = (block_of(target) + shards_of // 2) % shards_of
    return jnp.where((block_of(source) == first) | (block_of(source) == far), factor * values, values)


def shard_levels(rng, dims, cuts, smallest, top_value):
    factor_of = 1.0
    for dim, shards_of in cuts:
        steps = jax.random.uniform(jax.random.fold_in(jax.random.fold_in(rng, 6), dim), (shards_of,), jnp.float32, smallest / len(cuts), top_value / len(cuts))
        factor_of = factor_of * jnp.repeat(jnp.exp(steps), dims[dim] // shards_of).reshape((-1,) + (1,) * (len(dims) - 1 - dim))
    return factor_of


def gaussian_with(own_key, extent, deviation, most, pieces, heavy, kind=jnp.bfloat16):
    values = deviation * jax.random.normal(own_key, extent, jnp.float32)
    if pieces:
        values = values * shard_levels(own_key, extent, pieces, -0.22, 0.18)
    return jnp.clip(strengthened(values, jax.random.fold_in(own_key, 3), *heavy), -most, most).astype(kind)


def setup_inputs(seed: int = 0) -> dict:
    key_list = jax.random.split(jax.random.key(seed), 4)
    recording = draw_recording(jax.random.fold_in(key_list[3], 71), 0)
    shifts = draw_shifts(jax.random.fold_in(key_list[3], 71), 0)
    components = gaussian_with(key_list[2], (FRAMES, COMPONENT_COUNT), FRAMES ** -0.5, 0.3125, ((0, 4),), (0, 1, 4, 2.0))
    return dict(recording=recording, shifts=shifts, components=components)


def tap_weights(radius):
    return jnp.full((2 * radius + 1,), 1.0 / (2 * radius + 1), jnp.float32).astype(jnp.bfloat16)


def reference(recording, shifts, components):
    taps_wide = lax.optimization_barrier(tap_weights(RADIUS)).astype(jnp.float32)

    def filter_frame(inputs):
        picture, offset = inputs
        padded = jnp.pad(picture, SHIFT_MAX)
        registered = lax.dynamic_slice(padded, ((SHIFT_MAX - offset[0]).astype(jnp.int32), (SHIFT_MAX - offset[1]).astype(jnp.int32)), (HEIGHT, WIDTH))
        exact = registered.astype(jnp.float32)
        padded_rows = jnp.pad(exact, ((RADIUS, RADIUS), (0, 0)))
        rows_low = jnp.zeros((HEIGHT, WIDTH), jnp.float32)
        for position in range(2 * RADIUS + 1):
            rows_low = rows_low + taps_wide[position] * padded_rows[position:position + HEIGHT]
        rows_low = rows_low.astype(jnp.bfloat16)
        padded_cols = jnp.pad(rows_low.astype(jnp.float32), ((0, 0), (RADIUS, RADIUS)))
        lowpass = jnp.zeros((HEIGHT, WIDTH), jnp.float32)
        for position in range(2 * RADIUS + 1):
            lowpass = lowpass + taps_wide[position] * padded_cols[:, position:position + WIDTH]
        return (exact - lowpass).astype(jnp.bfloat16)

    filtered = lax.map(filter_frame, (recording, shifts))

    def project_rows(first_row):
        strip = lax.dynamic_slice_in_dim(filtered, first_row, TILE_ROWS, 1)
        flattened = strip.reshape(FRAMES_DEV * N_FR, TILE_ROWS * WIDTH)
        accumulated = jnp.zeros((COMPONENT_COUNT, TILE_ROWS * WIDTH), jnp.float32)
        for group_index in range(N_FR):
            low_edge = group_index * FRAMES_DEV
            block_sum = jnp.dot(components[low_edge:low_edge + FRAMES_DEV].T, flattened[low_edge:low_edge + FRAMES_DEV], preferred_element_type=jnp.float32)
            accumulated = accumulated + lax.optimization_barrier(block_sum.astype(jnp.bfloat16)).astype(jnp.float32)
        return accumulated.astype(jnp.bfloat16).reshape(COMPONENT_COUNT, TILE_ROWS, WIDTH)

    row_starts = (jnp.arange(N_PY) * TILE_ROWS).astype(jnp.int32)
    stacked = lax.map(project_rows, row_starts)
    return jnp.transpose(stacked, (1, 0, 2, 3)).reshape(COMPONENT_COUNT, HEIGHT, WIDTH)
```

```python
import jax
import jax.numpy as jnp
from jax import lax
from jax.experimental import pallas as pl
from jax.experimental.pallas import tpu as pltpu
from jax.sharding import PartitionSpec as P

SHIFT_MAX = 32
RADIUS = 4
CHUNKS = 2
HALO = SHIFT_MAX + RADIUS
SIDE = 40
PACK = 3


def rows_kernel(shift_ref, edge_ref, raw_ref, up_ref, down_ref, reg_ref, left_ref, right_ref, pad_ref):
    frames, rows, lanes = raw_ref.shape
    tall = rows + 2 * RADIUS
    index = lax.broadcasted_iota(jnp.int32, (tall, lanes), 0)
    lane = lax.broadcasted_iota(jnp.int32, (tall, lanes), 1)
    keep = (index >= edge_ref[0]) & (index < edge_ref[1])

    def group(g, count):
        lefts, rights = [], []
        for j in range(count):
            t = g * PACK + j
            pad_ref[j, 0:SIDE] = up_ref[t].astype(jnp.float32)
            pad_ref[j, SIDE : SIDE + rows] = raw_ref[t].astype(jnp.float32)
            pad_ref[j, SIDE + rows :] = down_ref[t].astype(jnp.float32)
            start = SIDE - RADIUS - shift_ref[t, 0]
            picked = jnp.where(keep, pad_ref[j, pl.ds(start, tall), :], 0.0)
            reg_ref[t] = picked.astype(jnp.bfloat16)
            lefts.append(picked if j == 0 else pltpu.roll(picked, HALO * j, 1))
            rights.append(pltpu.roll(picked, HALO * (j + 1), 1))
        left, right = lefts[0], rights[0]
        for j in range(1, count):
            left = jnp.where(lane < HALO * j, left, lefts[j])
            right = jnp.where(lane < HALO * j, right, rights[j])
        left_ref[g] = left.astype(jnp.bfloat16)
        right_ref[g] = right.astype(jnp.bfloat16)

    whole = frames // PACK
    lax.fori_loop(0, whole, lambda g, c: (group(g, PACK), c)[1], 0)
    if frames % PACK:
        group(whole, frames % PACK)


def columns_kernel(shift_ref, reg_ref, west_ref, east_ref, row_band_ref, col_band_ref, out_ref):
    frames, tall, lanes = reg_ref.shape
    rows = tall - 2 * RADIUS
    lane = lax.broadcasted_iota(jnp.int32, (tall, lanes), 1)

    def group(g, count):
        west = west_ref[g].astype(jnp.float32)
        east = east_ref[g].astype(jnp.float32)
        for j in range(count):
            t = g * PACK + j
            shift = shift_ref[t, 1]
            spot = (lanes - HALO * j) % lanes
            from_east = east if spot == 0 else pltpu.roll(east, spot, 1)
            from_west = pltpu.roll(west, (lanes - HALO - HALO * j) % lanes, 1)
            around = jnp.where(lane < lanes // 2, from_east, from_west)
            turn = (shift + lanes) & (lanes - 1)
            own = pltpu.roll(reg_ref[t].astype(jnp.float32), turn, 1)
            around = pltpu.roll(around, turn, 1)
            inside = (lane >= shift) & (lane < shift + lanes)
            mid = jnp.where(inside, own, around)
            rest = jnp.where(inside, around, own)
            window = jnp.concatenate([mid, rest], axis=1).astype(jnp.bfloat16)
            low = jnp.dot(row_band_ref[...], window, preferred_element_type=jnp.float32)
            low = jnp.dot(
                low.astype(jnp.bfloat16), col_band_ref[...], preferred_element_type=jnp.float32
            )
            out_ref[t] = (mid[RADIUS : RADIUS + rows] - low).astype(jnp.bfloat16)

    whole = frames // PACK
    lax.fori_loop(0, whole, lambda g, c: (group(g, PACK), c)[1], 0)
    if frames % PACK:
        group(whole, frames % PACK)


def tap():
    return jnp.float32(1.0 / (2 * RADIUS + 1))


def row_band(rows):
    shape = (rows, rows + 2 * RADIUS)
    offset = lax.broadcasted_iota(jnp.int32, shape, 1) - lax.broadcasted_iota(jnp.int32, shape, 0)
    return jnp.where((offset >= 0) & (offset <= 2 * RADIUS), tap(), 0.0).astype(jnp.bfloat16)


def col_band(cols, first, width):
    shape = (2 * cols, cols)
    spot = lax.broadcasted_iota(jnp.int32, shape, 0)
    col = jnp.where(spot >= cols + cols // 2, spot - 2 * cols, spot)
    near = jnp.abs(col - lax.broadcasted_iota(jnp.int32, shape, 1)) <= RADIUS
    there = (col + first >= 0) & (col + first < width)
    return jnp.where(near & there, tap(), 0.0).astype(jnp.bfloat16)


def moved(cells, axis, step):
    count = lax.axis_size(axis)
    pairs = [(i, i + step) for i in range(count) if 0 <= i + step < count]
    return lax.ppermute(cells, axis, pairs)


VMEM = pl.BlockSpec(memory_space=pltpu.VMEM)
SMEM = pl.BlockSpec(memory_space=pltpu.SMEM)
PARAMS = pltpu.CompilerParams(vmem_limit_bytes=40 * 1024 * 1024)


def body(recording, shifts, components):
    frames, rows, cols = recording.shape
    tall = rows + 2 * RADIUS
    part = frames // CHUNKS
    packs = -(-part // PACK)
    py, px = lax.axis_index("py"), lax.axis_index("px")
    height = rows * lax.axis_size("py")
    edge = jnp.stack([RADIUS - py * rows, RADIUS - py * rows + height]).astype(jnp.int32)
    bands = row_band(rows), col_band(cols, px * cols, cols * lax.axis_size("px"))
    filtered = []
    for c in range(CHUNKS):
        raw = recording[c * part : (c + 1) * part]
        shift = shifts[c * part : (c + 1) * part]
        up = moved(raw[:, rows - SIDE :], "py", 1)
        down = moved(raw[:, :SIDE], "py", -1)
        tile = jax.ShapeDtypeStruct((packs, tall, cols), jnp.bfloat16)
        reg, to_left, to_right = pl.pallas_call(
            rows_kernel,
            out_shape=(jax.ShapeDtypeStruct((part, tall, cols), jnp.bfloat16), tile, tile),
            in_specs=[SMEM, SMEM, VMEM, VMEM, VMEM],
            out_specs=(VMEM, VMEM, VMEM),
            scratch_shapes=[pltpu.VMEM((PACK, rows + 2 * SIDE, cols), jnp.float32)],
            compiler_params=PARAMS,
            cost_estimate=pl.CostEstimate(flops=10**9, bytes_accessed=10**7, transcendentals=0),
            name="rows",
        )(shift, edge, raw, up, down)
        east = moved(to_left, "px", -1)
        west = moved(to_right, "px", 1)
        filtered.append(
            pl.pallas_call(
                columns_kernel,
                out_shape=jax.ShapeDtypeStruct((part, rows, cols), jnp.bfloat16),
                in_specs=[SMEM, VMEM, VMEM, VMEM, VMEM, VMEM],
                out_specs=VMEM,
                compiler_params=PARAMS,
                cost_estimate=pl.CostEstimate(flops=10**9, bytes_accessed=10**7, transcendentals=0),
                name="columns",
            )(shift, reg, west, east, *bands)
        )
    filtered = jnp.concatenate(filtered, axis=0)
    partial = jnp.einsum(
        "fk,fij->kij", components, filtered, preferred_element_type=jnp.float32
    ).astype(jnp.bfloat16)
    return lax.psum_scatter(partial, "fr", scatter_dimension=0, tiled=True)


def solution(mesh):
    placed = (P("fr", "py", "px"), P("fr", None), P("fr", None))
    return jax.shard_map(
        body, mesh=mesh, in_specs=placed, out_specs=P("fr", "py", "px"), check_vma=False
    )
```

```python
import functools

import jax
import jax.numpy as jnp
from jax import lax
from jax.experimental import pallas as pl
from jax.experimental.pallas import tpu as pltpu
from jax.sharding import PartitionSpec as P

SHIFT_MAX = 32
RADIUS = 4
CHUNKS = 2
HALO = SHIFT_MAX + RADIUS
SIDE = 40
RING = 4
ROW_CHUNKS = 4
PACK = 3


def rows_kernel(shift_ref, edge_ref, raw_ref, up_ref, down_ref, reg_ref, left_ref, right_ref, pad_ref):
    frames, rows, lanes = raw_ref.shape
    tall = rows + 2 * RADIUS
    index = lax.broadcasted_iota(jnp.int32, (tall, lanes), 0)
    lane = lax.broadcasted_iota(jnp.int32, (tall, lanes), 1)
    keep = (index >= edge_ref[0]) & (index < edge_ref[1])

    def group(g, count):
        lefts, rights = [], []
        for j in range(count):
            t = g * PACK + j
            pad_ref[j, 0:SIDE] = up_ref[t].astype(jnp.float32)
            pad_ref[j, SIDE : SIDE + rows] = raw_ref[t].astype(jnp.float32)
            pad_ref[j, SIDE + rows :] = down_ref[t].astype(jnp.float32)
            start = SIDE - RADIUS - shift_ref[t, 0]
            picked = jnp.where(keep, pad_ref[j, pl.ds(start, tall), :], 0.0)
            reg_ref[t] = picked.astype(jnp.bfloat16)
            lefts.append(picked if j == 0 else pltpu.roll(picked, HALO * j, 1))
            rights.append(pltpu.roll(picked, HALO * (j + 1), 1))
        left, right = lefts[0], rights[0]
        for j in range(1, count):
            left = jnp.where(lane < HALO * j, left, lefts[j])
            right = jnp.where(lane < HALO * j, right, rights[j])
        left_ref[g] = left.astype(jnp.bfloat16)
        right_ref[g] = right.astype(jnp.bfloat16)

    whole = frames // PACK
    lax.fori_loop(0, whole, lambda g, c: (group(g, PACK), c)[1], 0)
    if frames % PACK:
        group(whole, frames % PACK)


def columns_kernel(
    shift_ref, turned_ref, reg_ref, west_ref, west_far_ref, east_ref, east_far_ref, row_band_ref, col_band_ref, out_ref
):
    frames, tall, lanes = reg_ref.shape
    rows = tall - 2 * RADIUS
    lane = lax.broadcasted_iota(jnp.int32, (tall, lanes), 1)

    def group(first, count):
        mids, lows = [], []
        for j in range(count):
            t = first + j
            if j % PACK == 0:
                g = (first + j) // PACK if isinstance(first, int) else lax.div(first, PACK) + j // PACK
                west = jnp.where(turned_ref[0] == 1, west_far_ref[g], west_ref[g]).astype(jnp.float32)
                east = jnp.where(turned_ref[1] == 1, east_far_ref[g], east_ref[g]).astype(jnp.float32)
            shift = shift_ref[t, 1]
            spot = (lanes - HALO * (j % PACK)) % lanes
            from_east = east if spot == 0 else pltpu.roll(east, spot, 1)
            from_west = pltpu.roll(west, (lanes - HALO - HALO * (j % PACK)) % lanes, 1)
            around = jnp.where(lane < lanes // 2, from_east, from_west)
            turn = (shift + lanes) & (lanes - 1)
            own = pltpu.roll(reg_ref[t].astype(jnp.float32), turn, 1)
            around = pltpu.roll(around, turn, 1)
            inside = (lane >= shift) & (lane < shift + lanes)
            mid = jnp.where(inside, own, around)
            rest = jnp.where(inside, around, own)
            window = jnp.concatenate([mid, rest], axis=1).astype(jnp.bfloat16)
            low = jnp.dot(row_band_ref[...], window, preferred_element_type=jnp.float32)
            mids.append(mid[RADIUS : RADIUS + rows])
            lows.append(low.astype(jnp.bfloat16))
        low = jnp.dot(
            jnp.concatenate(lows, axis=0), col_band_ref[...], preferred_element_type=jnp.float32
        )
        where = first * rows if isinstance(first, int) else pl.multiple_of(first * rows, rows)
        out_ref[pl.ds(where, count * rows), :] = jnp.concatenate(mids, axis=0) - low

    step = 2 * PACK
    whole = frames // step
    lax.fori_loop(0, whole, lambda g, c: (group(g * step, step), c)[1], 0)
    if frames % step:
        group(whole * step, frames % step)


def project_kernel(first, tile_rows, weight_ref, *refs):
    *parts, keep_ref, pass_ref, send_ref = refs
    count, comps, lanes = keep_ref.shape

    def one(i, carry):
        columns = [
            part[pl.ds(first + i, part.shape[0] // tile_rows, stride=tile_rows), :] for part in parts
        ]
        picture = jnp.concatenate(columns, axis=0).astype(jnp.bfloat16)
        total = jnp.dot(weight_ref[...], picture, preferred_element_type=jnp.float32)
        total = total.astype(jnp.bfloat16)
        keep_ref[i] = total[:comps]
        pass_ref[i] = total[comps : 2 * comps]
        send_ref[0, i] = total[2 * comps : 3 * comps]
        send_ref[1, i] = total[3 * comps :]
        return carry

    lax.fori_loop(0, count, one, 0)


def tap():
    return jnp.float32(1.0 / (2 * RADIUS + 1))


def row_band(rows):
    shape = (rows, rows + 2 * RADIUS)
    offset = lax.broadcasted_iota(jnp.int32, shape, 1) - lax.broadcasted_iota(jnp.int32, shape, 0)
    return jnp.where((offset >= 0) & (offset <= 2 * RADIUS), tap(), 0.0).astype(jnp.bfloat16)


def col_band(cols, first, width):
    shape = (2 * cols, cols)
    spot = lax.broadcasted_iota(jnp.int32, shape, 0)
    col = jnp.where(spot >= cols + cols // 2, spot - 2 * cols, spot)
    near = jnp.abs(col - lax.broadcasted_iota(jnp.int32, shape, 1)) <= RADIUS
    there = (col + first >= 0) & (col + first < width)
    return jnp.where(near & there, tap(), 0.0).astype(jnp.bfloat16)


def moved(cells, axis, step):
    count = lax.axis_size(axis)
    pairs = [(i, i + step) for i in range(count) if 0 <= i + step < count]
    return lax.ppermute(cells, axis, pairs)


def moved_px(cells, step, ring_first):
    count = lax.axis_size("px")
    ring = min(RING, count)
    last = ring - 1 if step == 1 else 0
    start = 0 if step == 1 else ring - 1
    around = [(i, i - i % ring + (i + step) % ring) for i in range(count)]
    def far(at):
        return [(i, i + step * ring) for i in range(at, count, ring) if 0 <= i + step * ring < count]
    if ring_first:
        near = lax.ppermute(cells, "px", around)
        return near, lax.ppermute(near, "px", far(start))
    landed = lax.ppermute(cells, "px", far(last))
    at_end = lax.axis_index("px") % ring == last
    near = lax.ppermute(jnp.where(at_end, landed, cells), "px", around)
    return near, near


VMEM = pl.BlockSpec(memory_space=pltpu.VMEM)
SMEM = pl.BlockSpec(memory_space=pltpu.SMEM)
PARAMS = pltpu.CompilerParams(vmem_limit_bytes=40 * 1024 * 1024)


def body(recording, shifts, components):
    frames, rows, cols = recording.shape
    tall = rows + 2 * RADIUS
    part = frames // CHUNKS
    packs = -(-part // PACK)
    py, px = lax.axis_index("py"), lax.axis_index("px")
    height = rows * lax.axis_size("py")
    edge = jnp.stack([RADIUS - py * rows, RADIUS - py * rows + height]).astype(jnp.int32)
    ring = min(RING, lax.axis_size("px"))
    turned = jnp.stack([px % ring == 0, px % ring == ring - 1]).astype(jnp.int32)
    bands = row_band(rows), col_band(cols, px * cols, cols * lax.axis_size("px"))
    filtered = []
    for c in range(CHUNKS):
        raw = recording[c * part : (c + 1) * part]
        shift = shifts[c * part : (c + 1) * part]
        up = moved(raw[:, rows - SIDE :], "py", 1)
        down = moved(raw[:, :SIDE], "py", -1)
        tile = jax.ShapeDtypeStruct((packs, tall, cols), jnp.bfloat16)
        reg, to_left, to_right = pl.pallas_call(
            rows_kernel,
            out_shape=(jax.ShapeDtypeStruct((part, tall, cols), jnp.bfloat16), tile, tile),
            in_specs=[SMEM, SMEM, VMEM, VMEM, VMEM],
            out_specs=(VMEM, VMEM, VMEM),
            scratch_shapes=[pltpu.VMEM((PACK, rows + 2 * SIDE, cols), jnp.float32)],
            compiler_params=PARAMS,
            cost_estimate=pl.CostEstimate(flops=10**9, bytes_accessed=10**7, transcendentals=0),
            name="rows",
        )(shift, edge, raw, up, down)
        east, east_far = moved_px(to_left, -1, c % 2 == 0)
        west, west_far = moved_px(to_right, 1, c % 2 == 0)
        filtered.append(
            pl.pallas_call(
                columns_kernel,
                out_shape=jax.ShapeDtypeStruct((part * rows, cols), jnp.float32),
                in_specs=[SMEM, SMEM] + [VMEM] * 7,
                out_specs=VMEM,
                compiler_params=PARAMS,
                cost_estimate=pl.CostEstimate(flops=10**9, bytes_accessed=10**7, transcendentals=0),
                name="columns",
            )(shift, turned, reg, west, west_far, east, east_far, *bands)
        )
    groups = lax.axis_size("fr")
    me = lax.axis_index("fr")
    comps = components.shape[1] // groups
    blocks = components.T.reshape(groups, comps, frames)
    weight = jnp.concatenate(
        [lax.dynamic_index_in_dim(blocks, me ^ k, 0, keepdims=False) for k in (0, 2, 1, 3)], axis=0
    )
    count = rows // ROW_CHUNKS
    block = jax.ShapeDtypeStruct((count, comps, cols), jnp.bfloat16)
    pair = jax.ShapeDtypeStruct((2, count, comps, cols), jnp.bfloat16)
    wide = jnp.float32
    done = []
    for c in range(ROW_CHUNKS):
        keep, onward, send = pl.pallas_call(
            functools.partial(project_kernel, c * count, rows),
            out_shape=(block, block, pair),
            in_specs=[VMEM] * (1 + CHUNKS),
            out_specs=(VMEM, VMEM, VMEM),
            compiler_params=PARAMS,
            cost_estimate=pl.CostEstimate(flops=10**9, bytes_accessed=10**7, transcendentals=0),
            name="project",
        )(weight, *filtered)
        near = lax.ppermute(send, "fr", [(i, i ^ 1) for i in range(groups)])
        onward = (onward.astype(wide) + near[1].astype(wide)).astype(jnp.bfloat16)
        far = lax.ppermute(onward, "fr", [(i, i ^ 2) for i in range(groups)])
        total = keep.astype(wide) + near[0].astype(wide) + far.astype(wide)
        done.append(total.astype(jnp.bfloat16))
    return jnp.concatenate(done, axis=0).transpose(1, 0, 2)


def solution(mesh):
    placed = (P("fr", "py", "px"), P("fr", None), P("fr", None))
    return jax.shard_map(
        body, mesh=mesh, in_specs=placed, out_specs=P("fr", "py", "px"), check_vma=False
    )
```

```python
import functools

import jax
import jax.numpy as jnp
from jax import lax
from jax.experimental import pallas as pl
from jax.experimental.pallas import tpu as pltpu
from jax.sharding import PartitionSpec as P

SHIFT_MAX = 32
RADIUS = 4
CHUNKS = 1
HALO = SHIFT_MAX + RADIUS
SIDE = 40
RING = 4
ROW_CHUNKS = 4
PACK = 3


def rows_kernel(shift_ref, edge_ref, raw_ref, up_ref, down_ref, reg_ref, left_ref, right_ref, pad_ref):
    frames, rows, lanes = raw_ref.shape
    tall = rows + 2 * RADIUS
    index = lax.broadcasted_iota(jnp.int32, (tall, lanes), 0)
    lane = lax.broadcasted_iota(jnp.int32, (tall, lanes), 1)
    keep = (index >= edge_ref[0]) & (index < edge_ref[1])

    def group(g, count):
        lefts, rights = [], []
        for j in range(count):
            t = g * PACK + j
            pad_ref[j, 0:SIDE] = up_ref[t].astype(jnp.float32)
            pad_ref[j, SIDE : SIDE + rows] = raw_ref[t].astype(jnp.float32)
            pad_ref[j, SIDE + rows :] = down_ref[t].astype(jnp.float32)
            start = SIDE - RADIUS - shift_ref[t, 0]
            picked = jnp.where(keep, pad_ref[j, pl.ds(start, tall), :], 0.0)
            reg_ref[t] = picked.astype(jnp.bfloat16)
            lefts.append(picked if j == 0 else pltpu.roll(picked, HALO * j, 1))
            rights.append(pltpu.roll(picked, HALO * (j + 1), 1))
        left, right = lefts[0], rights[0]
        for j in range(1, count):
            left = jnp.where(lane < HALO * j, left, lefts[j])
            right = jnp.where(lane < HALO * j, right, rights[j])
        left_ref[g] = left.astype(jnp.bfloat16)
        right_ref[g] = right.astype(jnp.bfloat16)

    whole = frames // PACK
    lax.fori_loop(0, whole, lambda g, c: (group(g, PACK), c)[1], 0)
    if frames % PACK:
        group(whole, frames % PACK)


def columns_kernel(shift_ref, reg_ref, west_ref, east_ref, row_band_ref, col_band_ref, out_ref):
    frames, tall, lanes = reg_ref.shape
    rows = tall - 2 * RADIUS
    lane = lax.broadcasted_iota(jnp.int32, (tall, lanes), 1)

    def group(first, count):
        mids, lows = [], []
        for j in range(count):
            t = first + j
            if j % PACK == 0:
                g = (first + j) // PACK if isinstance(first, int) else lax.div(first, PACK) + j // PACK
                west = west_ref[g].astype(jnp.float32)
                east = east_ref[g].astype(jnp.float32)
            shift = shift_ref[t, 1]
            spot = (lanes - HALO * (j % PACK)) % lanes
            from_east = east if spot == 0 else pltpu.roll(east, spot, 1)
            from_west = pltpu.roll(west, (lanes - HALO - HALO * (j % PACK)) % lanes, 1)
            around = jnp.where(lane < lanes // 2, from_east, from_west)
            turn = (shift + lanes) & (lanes - 1)
            own = pltpu.roll(reg_ref[t].astype(jnp.float32), turn, 1)
            around = pltpu.roll(around, turn, 1)
            inside = (lane >= shift) & (lane < shift + lanes)
            mid = jnp.where(inside, own, around)
            rest = jnp.where(inside, around, own)
            window = jnp.concatenate([mid, rest], axis=1).astype(jnp.bfloat16)
            low = jnp.dot(row_band_ref[...], window, preferred_element_type=jnp.float32)
            mids.append(mid[RADIUS : RADIUS + rows])
            lows.append(low.astype(jnp.bfloat16))
        low = jnp.dot(
            jnp.concatenate(lows, axis=0), col_band_ref[...], preferred_element_type=jnp.float32
        )
        where = first * rows if isinstance(first, int) else pl.multiple_of(first * rows, rows)
        out_ref[pl.ds(where, count * rows), :] = jnp.concatenate(mids, axis=0) - low

    step = 2 * PACK
    whole = frames // step
    lax.fori_loop(0, whole, lambda g, c: (group(g * step, step), c)[1], 0)
    if frames % step:
        group(whole * step, frames % step)


def project_kernel(first, tile_rows, weight_ref, *refs):
    *parts, keep_ref, pass_ref, send_ref = refs
    count, comps, lanes = keep_ref.shape

    def one(i, carry):
        columns = [
            part[pl.ds(first + i, part.shape[0] // tile_rows, stride=tile_rows), :] for part in parts
        ]
        picture = jnp.concatenate(columns, axis=0).astype(jnp.bfloat16)
        total = jnp.dot(weight_ref[...], picture, preferred_element_type=jnp.float32)
        total = total.astype(jnp.bfloat16)
        keep_ref[i] = total[:comps]
        pass_ref[i] = total[comps : 2 * comps]
        send_ref[0, i] = total[2 * comps : 3 * comps]
        send_ref[1, i] = total[3 * comps :]
        return carry

    lax.fori_loop(0, count, one, 0)


def tap():
    return jnp.float32(1.0 / (2 * RADIUS + 1))


def row_band(rows):
    shape = (rows, rows + 2 * RADIUS)
    offset = lax.broadcasted_iota(jnp.int32, shape, 1) - lax.broadcasted_iota(jnp.int32, shape, 0)
    return jnp.where((offset >= 0) & (offset <= 2 * RADIUS), tap(), 0.0).astype(jnp.bfloat16)


def col_band(cols, first, width):
    shape = (2 * cols, cols)
    spot = lax.broadcasted_iota(jnp.int32, shape, 0)
    col = jnp.where(spot >= cols + cols // 2, spot - 2 * cols, spot)
    near = jnp.abs(col - lax.broadcasted_iota(jnp.int32, shape, 1)) <= RADIUS
    there = (col + first >= 0) & (col + first < width)
    return jnp.where(near & there, tap(), 0.0).astype(jnp.bfloat16)


def moved(cells, axis, step):
    count = lax.axis_size(axis)
    pairs = [(i, i + step) for i in range(count) if 0 <= i + step < count]
    return lax.ppermute(cells, axis, pairs)


def exchange_kernel(
    to_left, to_right, west, east, hop, second, plain_out, plain_in, out_1, in_1, out_2, in_2, out_3, in_3
):
    count = lax.axis_size("px")
    me = lax.axis_index("px")
    spot, ring = lax.rem(me, RING), lax.div(me, RING)
    rings = count // RING
    packs = to_left.shape[0]
    cuts = [packs * k // 6 for k in range(7)]
    lots = [(0, 1), (2,), (3,), (4, 5)]

    def piece(ref, k):
        return ref.at[pl.ds(cuts[k], cuts[k + 1] - cuts[k])]

    def kept(ref, d, i, k):
        return ref.at[d, i, pl.ds(0, cuts[k + 1] - cuts[k])]

    def copy(source, target, sent, got, px):
        return pltpu.make_async_remote_copy(
            src_ref=source,
            dst_ref=target,
            send_sem=sent,
            recv_sem=got,
            device_id={"px": px},
            device_id_type=pl.DeviceIdType.MESH,
        )

    barrier = pltpu.get_barrier_semaphore()
    for k in range(1, RING):
        pl.semaphore_signal(
            barrier,
            inc=1,
            device_id={"px": ring * RING + lax.rem(spot + k, RING)},
            device_id_type=pl.DeviceIdType.MESH,
        )
    for step in (1, -1):
        @pl.when((ring + step >= 0) & (ring + step < rings))
        def _():
            pl.semaphore_signal(
                barrier,
                inc=1,
                device_id={"px": me + step * RING},
                device_id_type=pl.DeviceIdType.MESH,
            )
    at_end = (ring == 0) | (ring == rings - 1)

    @pl.when(at_end)
    def _():
        pl.semaphore_wait(barrier, RING)

    @pl.when(jnp.logical_not(at_end))
    def _():
        pl.semaphore_wait(barrier, RING + 1)

    sides = []
    for d, step, source, target, first, final in (
        (0, 1, to_right, west, RING - 1, 0),
        (1, -1, to_left, east, 0, RING - 1),
    ):
        onward = (ring + step >= 0) & (ring + step < rings)
        arriving = (ring - step >= 0) & (ring - step < rings)

        def plain(d=d, step=step, source=source, target=target):
            return copy(source, target, plain_out.at[d], plain_in.at[d], me + step)

        def spread(c, i, k, d=d, source=source):
            return copy(
                piece(source, k), kept(hop, d, i, k), out_1.at[d, c, i], in_1.at[d, i], ring * RING + c
            )

        def cross(c, i, k, d=d, step=step, source=source, target=target, first=first, final=final):
            return copy(
                piece(source, k) if c == first else kept(hop, d, i, k),
                piece(target, k) if c == final else kept(second, d, i, k),
                out_2.at[d, i],
                in_2.at[d, i],
                me + step * RING,
            )

        def gather(c, i, k, d=d, target=target, final=final):
            return copy(
                kept(second, d, i, k),
                piece(target, k),
                out_3.at[d, i],
                in_3.at[d, c, i],
                ring * RING + final,
            )

        sides.append((target, first, final, onward, arriving, plain, spread, cross, gather))

    def each(c):
        return list(enumerate(lots[c]))

    for target, first, final, onward, arriving, plain, spread, cross, gather in sides:
        @pl.when((spot == first) & onward)
        def _():
            for i, k in each(first):
                cross(first, i, k).start()
            for c in range(RING):
                if c != first:
                    for i, k in each(c):
                        spread(c, i, k).start()

        @pl.when(spot != first)
        def _():
            plain().start()

    for c in range(RING):
        for target, first, final, onward, arriving, plain, spread, cross, gather in sides:
            if c != first:
                @pl.when((spot == c) & onward)
                def _():
                    for i, k in each(c):
                        spread(c, i, k).wait_recv()
                        cross(c, i, k).start()

    for c in range(RING):
        for target, first, final, onward, arriving, plain, spread, cross, gather in sides:
            if c != final:
                @pl.when((spot == c) & arriving)
                def _():
                    for i, k in each(c):
                        cross(c, i, k).wait_recv()
                        gather(c, i, k).start()

    for target, first, final, onward, arriving, plain, spread, cross, gather in sides:
        @pl.when((spot == final) & arriving)
        def _():
            for c in range(RING):
                for i, k in each(c):
                    (cross if c == final else gather)(c, i, k).wait_recv()

        @pl.when((spot == final) & jnp.logical_not(arriving))
        def _():
            target[...] = jnp.zeros_like(target)

        @pl.when(spot != final)
        def _():
            plain().wait_recv()

    for target, first, final, onward, arriving, plain, spread, cross, gather in sides:
        @pl.when((spot == first) & onward)
        def _():
            for c in range(RING):
                if c != first:
                    for i, k in each(c):
                        spread(c, i, k).wait_send()

        @pl.when(spot != first)
        def _():
            plain().wait_send()

        for c in range(RING):
            @pl.when((spot == c) & onward)
            def _():
                for i, k in each(c):
                    cross(c, i, k).wait_send()

            if c != final:
                @pl.when((spot == c) & arriving)
                def _():
                    for i, k in each(c):
                        gather(c, i, k).wait_send()


def exchanged(to_left, to_right):
    tile = jax.ShapeDtypeStruct(to_left.shape, to_left.dtype)
    packs = to_left.shape[0]
    kept = pltpu.VMEM((2, 2, -(-packs // 6)) + to_left.shape[1:], to_left.dtype)
    sem = pltpu.SemaphoreType.DMA
    return pl.pallas_call(
        exchange_kernel,
        out_shape=(tile, tile),
        in_specs=[VMEM, VMEM],
        out_specs=(VMEM, VMEM),
        scratch_shapes=[kept, kept, sem((2,)), sem((2,)), sem((2, RING, 2)), sem((2, 2))]
        + [sem((2, 2)), sem((2, 2)), sem((2, 2)), sem((2, RING, 2))],
        compiler_params=pltpu.CompilerParams(
            vmem_limit_bytes=24 * 1024 * 1024, collective_id=0, has_side_effects=True
        ),
        name="exchange",
    )(to_left, to_right)


VMEM = pl.BlockSpec(memory_space=pltpu.VMEM)
SMEM = pl.BlockSpec(memory_space=pltpu.SMEM)
PARAMS = pltpu.CompilerParams(vmem_limit_bytes=40 * 1024 * 1024)


def body(recording, shifts, components):
    frames, rows, cols = recording.shape
    tall = rows + 2 * RADIUS
    part = frames // CHUNKS
    packs = -(-part // PACK)
    py, px = lax.axis_index("py"), lax.axis_index("px")
    height = rows * lax.axis_size("py")
    edge = jnp.stack([RADIUS - py * rows, RADIUS - py * rows + height]).astype(jnp.int32)
    bands = row_band(rows), col_band(cols, px * cols, cols * lax.axis_size("px"))
    filtered = []
    for c in range(CHUNKS):
        raw = recording[c * part : (c + 1) * part]
        shift = shifts[c * part : (c + 1) * part]
        up = moved(raw[:, rows - SIDE :], "py", 1)
        down = moved(raw[:, :SIDE], "py", -1)
        tile = jax.ShapeDtypeStruct((packs, tall, cols), jnp.bfloat16)
        reg, to_left, to_right = pl.pallas_call(
            rows_kernel,
            out_shape=(jax.ShapeDtypeStruct((part, tall, cols), jnp.bfloat16), tile, tile),
            in_specs=[SMEM, SMEM, VMEM, VMEM, VMEM],
            out_specs=(VMEM, VMEM, VMEM),
            scratch_shapes=[pltpu.VMEM((PACK, rows + 2 * SIDE, cols), jnp.float32)],
            compiler_params=PARAMS,
            cost_estimate=pl.CostEstimate(flops=10**9, bytes_accessed=10**7, transcendentals=0),
            name="rows",
        )(shift, edge, raw, up, down)
        west, east = exchanged(to_left, to_right)
        filtered.append(
            pl.pallas_call(
                columns_kernel,
                out_shape=jax.ShapeDtypeStruct((part * rows, cols), jnp.float32),
                in_specs=[SMEM] + [VMEM] * 5,
                out_specs=VMEM,
                compiler_params=PARAMS,
                cost_estimate=pl.CostEstimate(flops=10**9, bytes_accessed=10**7, transcendentals=0),
                name="columns",
            )(shift, reg, west, east, *bands)
        )
    groups = lax.axis_size("fr")
    me = lax.axis_index("fr")
    comps = components.shape[1] // groups
    blocks = components.T.reshape(groups, comps, frames)
    weight = jnp.concatenate(
        [lax.dynamic_index_in_dim(blocks, me ^ k, 0, keepdims=False) for k in (0, 2, 1, 3)], axis=0
    )
    count = rows // ROW_CHUNKS
    block = jax.ShapeDtypeStruct((count, comps, cols), jnp.bfloat16)
    pair = jax.ShapeDtypeStruct((2, count, comps, cols), jnp.bfloat16)
    wide = jnp.float32
    done = []
    for c in range(ROW_CHUNKS):
        keep, onward, send = pl.pallas_call(
            functools.partial(project_kernel, c * count, rows),
            out_shape=(block, block, pair),
            in_specs=[VMEM] * (1 + CHUNKS),
            out_specs=(VMEM, VMEM, VMEM),
            compiler_params=PARAMS,
            cost_estimate=pl.CostEstimate(flops=10**9, bytes_accessed=10**7, transcendentals=0),
            name="project",
        )(weight, *filtered)
        near = lax.ppermute(send, "fr", [(i, i ^ 1) for i in range(groups)])
        onward = (onward.astype(wide) + near[1].astype(wide)).astype(jnp.bfloat16)
        far = lax.ppermute(onward, "fr", [(i, i ^ 2) for i in range(groups)])
        total = keep.astype(wide) + near[0].astype(wide) + far.astype(wide)
        done.append(total.astype(jnp.bfloat16))
    return jnp.concatenate(done, axis=0).transpose(1, 0, 2)


def solution(mesh):
    placed = (P("fr", "py", "px"), P("fr", None), P("fr", None))
    return jax.shard_map(
        body, mesh=mesh, in_specs=placed, out_specs=P("fr", "py", "px"), check_vma=False
    )
```

```python
import functools

import jax
import jax.numpy as jnp
from jax import lax
from jax.experimental import pallas as pl
from jax.experimental.pallas import tpu as pltpu
from jax.sharding import PartitionSpec as P

SHIFT_MAX = 32
RADIUS = 4
CHUNKS = 1
HALO = SHIFT_MAX + RADIUS
SIDE = 40
RING = 4
ROW_CHUNKS = 4
UNROLL = 4
PACK = 3


def rows_kernel(shift_ref, edge_ref, raw_ref, up_ref, down_ref, reg_ref, left_ref, right_ref, pad_ref):
    frames, rows, lanes = raw_ref.shape
    tall = rows + 2 * RADIUS
    index = lax.broadcasted_iota(jnp.int32, (tall, lanes), 0)
    lane = lax.broadcasted_iota(jnp.int32, (tall, lanes), 1)
    keep = (index >= edge_ref[0]) & (index < edge_ref[1])

    def group(g, count):
        lefts, rights = [], []
        for j in range(count):
            t = g * PACK + j
            pad_ref[j, 0:SIDE] = up_ref[t].astype(jnp.float32)
            pad_ref[j, SIDE : SIDE + rows] = raw_ref[t].astype(jnp.float32)
            pad_ref[j, SIDE + rows :] = down_ref[t].astype(jnp.float32)
            start = SIDE - RADIUS - shift_ref[t, 0]
            picked = jnp.where(keep, pad_ref[j, pl.ds(start, tall), :], 0.0)
            reg_ref[t] = picked.astype(jnp.bfloat16)
            lefts.append(picked if j == 0 else pltpu.roll(picked, HALO * j, 1))
            rights.append(pltpu.roll(picked, HALO * (j + 1), 1))
        left, right = lefts[0], rights[0]
        for j in range(1, count):
            left = jnp.where(lane < HALO * j, left, lefts[j])
            right = jnp.where(lane < HALO * j, right, rights[j])
        left_ref[g] = left.astype(jnp.bfloat16)
        right_ref[g] = right.astype(jnp.bfloat16)

    whole = frames // PACK
    lax.fori_loop(0, whole, lambda g, c: (group(g, PACK), c)[1], 0)
    if frames % PACK:
        group(whole, frames % PACK)


def columns_kernel(shift_ref, reg_ref, west_ref, east_ref, row_band_ref, col_band_ref, out_ref):
    frames, tall, lanes = reg_ref.shape
    rows = tall - 2 * RADIUS
    lane = lax.broadcasted_iota(jnp.int32, (tall, lanes), 1)

    def group(first, count):
        mids, lows = [], []
        for j in range(count):
            t = first + j
            if j % PACK == 0:
                g = (first + j) // PACK if isinstance(first, int) else lax.div(first, PACK) + j // PACK
                west = west_ref[g].astype(jnp.float32)
                east = east_ref[g].astype(jnp.float32)
            shift = shift_ref[t, 1]
            spot = (lanes - HALO * (j % PACK)) % lanes
            from_east = east if spot == 0 else pltpu.roll(east, spot, 1)
            from_west = pltpu.roll(west, (lanes - HALO - HALO * (j % PACK)) % lanes, 1)
            around = jnp.where(lane < lanes // 2, from_east, from_west)
            turn = (shift + lanes) & (lanes - 1)
            own = pltpu.roll(reg_ref[t].astype(jnp.float32), turn, 1)
            around = pltpu.roll(around, turn, 1)
            inside = (lane >= shift) & (lane < shift + lanes)
            mid = jnp.where(inside, own, around)
            rest = jnp.where(inside, around, own)
            window = jnp.concatenate([mid, rest], axis=1).astype(jnp.bfloat16)
            low = jnp.dot(row_band_ref[...], window, preferred_element_type=jnp.float32)
            mids.append(mid[RADIUS : RADIUS + rows])
            lows.append(low.astype(jnp.bfloat16))
        low = jnp.dot(
            jnp.concatenate(lows, axis=0), col_band_ref[...], preferred_element_type=jnp.float32
        )
        where = first * rows if isinstance(first, int) else pl.multiple_of(first * rows, rows)
        out_ref[pl.ds(where, count * rows), :] = jnp.concatenate(mids, axis=0) - low

    step = 2 * PACK
    whole = frames // step
    lax.fori_loop(0, whole, lambda g, c: (group(g * step, step), c)[1], 0)
    if frames % step:
        group(whole * step, frames % step)


def project_kernel(first, tile_rows, weight_ref, *refs):
    *parts, keep_ref, pass_ref, send_ref = refs
    count, comps, lanes = keep_ref.shape

    def some(g, carry):
        for j in range(UNROLL):
            i = g * UNROLL + j
            columns = [
                part[pl.ds(first + i, part.shape[0] // tile_rows, stride=tile_rows), :]
                for part in parts
            ]
            picture = jnp.concatenate(columns, axis=0).astype(jnp.bfloat16)
            total = jnp.dot(weight_ref[...], picture, preferred_element_type=jnp.float32)
            total = total.astype(jnp.bfloat16)
            keep_ref[i] = total[:comps]
            pass_ref[i] = total[comps : 2 * comps]
            send_ref[0, i] = total[2 * comps : 3 * comps]
            send_ref[1, i] = total[3 * comps :]
        return carry

    lax.fori_loop(0, count // UNROLL, some, 0)


def tap():
    return jnp.float32(1.0 / (2 * RADIUS + 1))


def row_band(rows):
    shape = (rows, rows + 2 * RADIUS)
    offset = lax.broadcasted_iota(jnp.int32, shape, 1) - lax.broadcasted_iota(jnp.int32, shape, 0)
    return jnp.where((offset >= 0) & (offset <= 2 * RADIUS), tap(), 0.0).astype(jnp.bfloat16)


def col_band(cols, first, width):
    shape = (2 * cols, cols)
    spot = lax.broadcasted_iota(jnp.int32, shape, 0)
    col = jnp.where(spot >= cols + cols // 2, spot - 2 * cols, spot)
    near = jnp.abs(col - lax.broadcasted_iota(jnp.int32, shape, 1)) <= RADIUS
    there = (col + first >= 0) & (col + first < width)
    return jnp.where(near & there, tap(), 0.0).astype(jnp.bfloat16)


def sides_kernel(raw, up, down, out_sem, in_sem):
    rows = raw.shape[1]
    count = lax.axis_size("py")
    me = lax.axis_index("py")
    has_up, has_down = me > 0, me < count - 1
    barrier = pltpu.get_barrier_semaphore()

    for there, step in ((has_up, -1), (has_down, 1)):
        @pl.when(there)
        def _():
            pl.semaphore_signal(
                barrier, inc=1, device_id={"py": me + step}, device_id_type=pl.DeviceIdType.MESH
            )

    both = has_up & has_down

    @pl.when(both)
    def _():
        pl.semaphore_wait(barrier, 2)

    @pl.when(jnp.logical_not(both))
    def _():
        pl.semaphore_wait(barrier, 1)

    moves = []
    for d, (sends, gets, step, first, target) in enumerate(
        ((has_down, has_up, 1, rows - SIDE, up), (has_up, has_down, -1, 0, down))
    ):
        def move(d=d, step=step, first=first, target=target):
            return pltpu.make_async_remote_copy(
                src_ref=raw.at[:, pl.ds(first, SIDE)],
                dst_ref=target,
                send_sem=out_sem.at[d],
                recv_sem=in_sem.at[d],
                device_id={"py": me + step},
                device_id_type=pl.DeviceIdType.MESH,
            )

        moves.append((sends, gets, target, move))

    for sends, gets, target, move in moves:
        @pl.when(sends)
        def _():
            move().start()

    for sends, gets, target, move in moves:
        @pl.when(jnp.logical_not(gets))
        def _():
            target[...] = jnp.zeros_like(target)

    for sends, gets, target, move in moves:
        @pl.when(gets)
        def _():
            move().wait_recv()

    for sends, gets, target, move in moves:
        @pl.when(sends)
        def _():
            move().wait_send()


def sides_of(raw):
    frames, _, cols = raw.shape
    side = jax.ShapeDtypeStruct((frames, SIDE, cols), raw.dtype)
    return pl.pallas_call(
        sides_kernel,
        out_shape=(side, side),
        in_specs=[pl.BlockSpec(memory_space=pl.ANY)],
        out_specs=(VMEM, VMEM),
        scratch_shapes=[pltpu.SemaphoreType.DMA((2,)), pltpu.SemaphoreType.DMA((2,))],
        compiler_params=pltpu.CompilerParams(
            vmem_limit_bytes=24 * 1024 * 1024, collective_id=1, has_side_effects=True
        ),
        name="sides",
    )(raw)


def exchange_kernel(
    to_left, to_right, west, east, hop, second, plain_out, plain_in, out_1, in_1, out_2, in_2, out_3, in_3
):
    count = lax.axis_size("px")
    me = lax.axis_index("px")
    spot, ring = lax.rem(me, RING), lax.div(me, RING)
    rings = count // RING
    packs = to_left.shape[0]
    cuts = [packs * k // 12 for k in range(13)]
    lots = [(0, 1, 2, 3), (4, 5), (6, 7), (8, 9, 10, 11)]

    def piece(ref, k):
        return ref.at[pl.ds(cuts[k], cuts[k + 1] - cuts[k])]

    def kept(ref, d, i, k):
        return ref.at[d, i, pl.ds(0, cuts[k + 1] - cuts[k])]

    def copy(source, target, sent, got, px):
        return pltpu.make_async_remote_copy(
            src_ref=source,
            dst_ref=target,
            send_sem=sent,
            recv_sem=got,
            device_id={"px": px},
            device_id_type=pl.DeviceIdType.MESH,
        )

    barrier = pltpu.get_barrier_semaphore()
    for k in range(1, RING):
        pl.semaphore_signal(
            barrier,
            inc=1,
            device_id={"px": ring * RING + lax.rem(spot + k, RING)},
            device_id_type=pl.DeviceIdType.MESH,
        )
    for step in (1, -1):
        @pl.when((ring + step >= 0) & (ring + step < rings))
        def _():
            pl.semaphore_signal(
                barrier,
                inc=1,
                device_id={"px": me + step * RING},
                device_id_type=pl.DeviceIdType.MESH,
            )
    at_end = (ring == 0) | (ring == rings - 1)

    @pl.when(at_end)
    def _():
        pl.semaphore_wait(barrier, RING)

    @pl.when(jnp.logical_not(at_end))
    def _():
        pl.semaphore_wait(barrier, RING + 1)

    sides = []
    for d, step, source, target, first, final in (
        (0, 1, to_right, west, RING - 1, 0),
        (1, -1, to_left, east, 0, RING - 1),
    ):
        onward = (ring + step >= 0) & (ring + step < rings)
        arriving = (ring - step >= 0) & (ring - step < rings)

        def plain(d=d, step=step, source=source, target=target):
            return copy(source, target, plain_out.at[d], plain_in.at[d], me + step)

        def spread(c, i, k, d=d, source=source):
            return copy(
                piece(source, k), kept(hop, d, i, k), out_1.at[d, c, i], in_1.at[d, i], ring * RING + c
            )

        def cross(c, i, k, d=d, step=step, source=source, target=target, first=first, final=final):
            return copy(
                piece(source, k) if c == first else kept(hop, d, i, k),
                piece(target, k) if c == final else kept(second, d, i, k),
                out_2.at[d, i],
                in_2.at[d, i],
                me + step * RING,
            )

        def gather(c, i, k, d=d, target=target, final=final):
            return copy(
                kept(second, d, i, k),
                piece(target, k),
                out_3.at[d, i],
                in_3.at[d, c, i],
                ring * RING + final,
            )

        sides.append((target, first, final, onward, arriving, plain, spread, cross, gather))

    def each(c):
        return list(enumerate(lots[c]))

    for target, first, final, onward, arriving, plain, spread, cross, gather in sides:
        @pl.when((spot == first) & onward)
        def _():
            for i, k in each(first):
                cross(first, i, k).start()
            for c in range(RING):
                if c != first:
                    for i, k in each(c):
                        spread(c, i, k).start()

    for c in range(RING):
        for i, k in each(c):
            for target, first, final, onward, arriving, plain, spread, cross, gather in sides:
                if c != first:
                    @pl.when((spot == c) & onward)
                    def _():
                        spread(c, i, k).wait_recv()
                        cross(c, i, k).start()

    for target, first, final, onward, arriving, plain, spread, cross, gather in sides:
        @pl.when(spot != first)
        def _():
            plain().start()

    for c in range(RING):
        for i, k in each(c):
            for target, first, final, onward, arriving, plain, spread, cross, gather in sides:
                if c != final:
                    @pl.when((spot == c) & arriving)
                    def _():
                        cross(c, i, k).wait_recv()
                        gather(c, i, k).start()

    for target, first, final, onward, arriving, plain, spread, cross, gather in sides:
        @pl.when((spot == final) & arriving)
        def _():
            for c in range(RING):
                for i, k in each(c):
                    (cross if c == final else gather)(c, i, k).wait_recv()

        @pl.when((spot == final) & jnp.logical_not(arriving))
        def _():
            target[...] = jnp.zeros_like(target)

        @pl.when(spot != final)
        def _():
            plain().wait_recv()

    for target, first, final, onward, arriving, plain, spread, cross, gather in sides:
        @pl.when((spot == first) & onward)
        def _():
            for c in range(RING):
                if c != first:
                    for i, k in each(c):
                        spread(c, i, k).wait_send()

        @pl.when(spot != first)
        def _():
            plain().wait_send()

        for c in range(RING):
            @pl.when((spot == c) & onward)
            def _():
                for i, k in each(c):
                    cross(c, i, k).wait_send()

            if c != final:
                @pl.when((spot == c) & arriving)
                def _():
                    for i, k in each(c):
                        gather(c, i, k).wait_send()


def exchanged(to_left, to_right):
    tile = jax.ShapeDtypeStruct(to_left.shape, to_left.dtype)
    packs = to_left.shape[0]
    kept = pltpu.VMEM((2, 4, -(-packs // 12)) + to_left.shape[1:], to_left.dtype)
    sem = pltpu.SemaphoreType.DMA
    return pl.pallas_call(
        exchange_kernel,
        out_shape=(tile, tile),
        in_specs=[VMEM, VMEM],
        out_specs=(VMEM, VMEM),
        scratch_shapes=[kept, kept, sem((2,)), sem((2,)), sem((2, RING, 4)), sem((2, 4))]
        + [sem((2, 4)), sem((2, 4)), sem((2, 4)), sem((2, RING, 4))],
        compiler_params=pltpu.CompilerParams(
            vmem_limit_bytes=24 * 1024 * 1024, collective_id=0, has_side_effects=True
        ),
        name="exchange",
    )(to_left, to_right)


VMEM = pl.BlockSpec(memory_space=pltpu.VMEM)
SMEM = pl.BlockSpec(memory_space=pltpu.SMEM)
PARAMS = pltpu.CompilerParams(vmem_limit_bytes=40 * 1024 * 1024)


def body(recording, shifts, components):
    frames, rows, cols = recording.shape
    tall = rows + 2 * RADIUS
    part = frames // CHUNKS
    packs = -(-part // PACK)
    py, px = lax.axis_index("py"), lax.axis_index("px")
    height = rows * lax.axis_size("py")
    edge = jnp.stack([RADIUS - py * rows, RADIUS - py * rows + height]).astype(jnp.int32)
    bands = row_band(rows), col_band(cols, px * cols, cols * lax.axis_size("px"))
    filtered = []
    for c in range(CHUNKS):
        raw = recording[c * part : (c + 1) * part]
        shift = shifts[c * part : (c + 1) * part]
        up, down = sides_of(raw)
        tile = jax.ShapeDtypeStruct((packs, tall, cols), jnp.bfloat16)
        reg, to_left, to_right = pl.pallas_call(
            rows_kernel,
            out_shape=(jax.ShapeDtypeStruct((part, tall, cols), jnp.bfloat16), tile, tile),
            in_specs=[SMEM, SMEM, VMEM, VMEM, VMEM],
            out_specs=(VMEM, VMEM, VMEM),
            scratch_shapes=[pltpu.VMEM((PACK, rows + 2 * SIDE, cols), jnp.float32)],
            compiler_params=PARAMS,
            cost_estimate=pl.CostEstimate(flops=10**9, bytes_accessed=10**7, transcendentals=0),
            name="rows",
        )(shift, edge, raw, up, down)
        west, east = exchanged(to_left, to_right)
        filtered.append(
            pl.pallas_call(
                columns_kernel,
                out_shape=jax.ShapeDtypeStruct((part * rows, cols), jnp.float32),
                in_specs=[SMEM] + [VMEM] * 5,
                out_specs=VMEM,
                compiler_params=PARAMS,
                cost_estimate=pl.CostEstimate(flops=10**9, bytes_accessed=10**7, transcendentals=0),
                name="columns",
            )(shift, reg, west, east, *bands)
        )
    groups = lax.axis_size("fr")
    me = lax.axis_index("fr")
    comps = components.shape[1] // groups
    blocks = components.T.reshape(groups, comps, frames)
    weight = jnp.concatenate(
        [lax.dynamic_index_in_dim(blocks, me ^ k, 0, keepdims=False) for k in (0, 2, 1, 3)], axis=0
    )
    count = rows // ROW_CHUNKS
    block = jax.ShapeDtypeStruct((count, comps, cols), jnp.bfloat16)
    pair = jax.ShapeDtypeStruct((2, count, comps, cols), jnp.bfloat16)
    wide = jnp.float32
    done = []
    for c in range(ROW_CHUNKS):
        keep, onward, send = pl.pallas_call(
            functools.partial(project_kernel, c * count, rows),
            out_shape=(block, block, pair),
            in_specs=[VMEM] * (1 + CHUNKS),
            out_specs=(VMEM, VMEM, VMEM),
            compiler_params=PARAMS,
            cost_estimate=pl.CostEstimate(flops=10**9, bytes_accessed=10**7, transcendentals=0),
            name="project",
        )(weight, *filtered)
        near = lax.ppermute(send, "fr", [(i, i ^ 1) for i in range(groups)])
        onward = (onward.astype(wide) + near[1].astype(wide)).astype(jnp.bfloat16)
        far = lax.ppermute(onward, "fr", [(i, i ^ 2) for i in range(groups)])
        total = keep.astype(wide) + near[0].astype(wide) + far.astype(wide)
        done.append(total.astype(jnp.bfloat16))
    return jnp.concatenate(done, axis=0).transpose(1, 0, 2)


def solution(mesh):
    placed = (P("fr", "py", "px"), P("fr", None), P("fr", None))
    return jax.shard_map(
        body, mesh=mesh, in_specs=placed, out_specs=P("fr", "py", "px"), check_vma=False
    )
```

```python
import functools

import jax
import jax.numpy as jnp
from jax import lax
from jax.experimental import pallas as pl
from jax.experimental.pallas import tpu as pltpu
from jax.sharding import PartitionSpec as P

SHIFT_MAX = 32
RADIUS = 4
CHUNKS = 1
HALO = SHIFT_MAX + RADIUS
SIDE = 40
RING = 4
ROW_CHUNKS = 4
UNROLL = 4
PACK = 3


def rows_kernel(shift_ref, edge_ref, raw_ref, up_ref, down_ref, reg_ref, left_ref, right_ref, pad_ref):
    frames, rows, lanes = raw_ref.shape
    tall = rows + 2 * RADIUS
    index = lax.broadcasted_iota(jnp.int32, (tall, lanes), 0)
    lane = lax.broadcasted_iota(jnp.int32, (tall, lanes), 1)
    keep = (index >= edge_ref[0]) & (index < edge_ref[1])

    def group(g, count):
        lefts, rights = [], []
        for j in range(count):
            t = g * PACK + j
            pad_ref[j, 0:SIDE] = up_ref[t].astype(jnp.float32)
            pad_ref[j, SIDE : SIDE + rows] = raw_ref[t].astype(jnp.float32)
            pad_ref[j, SIDE + rows :] = down_ref[t].astype(jnp.float32)
            start = SIDE - RADIUS - shift_ref[t, 0]
            picked = jnp.where(keep, pad_ref[j, pl.ds(start, tall), :], 0.0)
            reg_ref[t] = picked.astype(jnp.bfloat16)
            lefts.append(picked if j == 0 else pltpu.roll(picked, HALO * j, 1))
            rights.append(pltpu.roll(picked, HALO * (j + 1), 1))
        left, right = lefts[0], rights[0]
        for j in range(1, count):
            left = jnp.where(lane < HALO * j, left, lefts[j])
            right = jnp.where(lane < HALO * j, right, rights[j])
        left_ref[g] = left.astype(jnp.bfloat16)
        right_ref[g] = right.astype(jnp.bfloat16)

    whole = frames // PACK
    lax.fori_loop(0, whole, lambda g, c: (group(g, PACK), c)[1], 0)
    if frames % PACK:
        group(whole, frames % PACK)


def columns_kernel(shift_ref, reg_ref, west_ref, east_ref, row_band_ref, col_band_ref, out_ref):
    frames, tall, lanes = reg_ref.shape
    rows = tall - 2 * RADIUS
    lane = lax.broadcasted_iota(jnp.int32, (tall, lanes), 1)

    def group(first, count):
        mids, lows = [], []
        for j in range(count):
            t = first + j
            if j % PACK == 0:
                g = (first + j) // PACK if isinstance(first, int) else lax.div(first, PACK) + j // PACK
                west = west_ref[g].astype(jnp.float32)
                east = east_ref[g].astype(jnp.float32)
            shift = shift_ref[t, 1]
            spot = (lanes - HALO * (j % PACK)) % lanes
            from_east = east if spot == 0 else pltpu.roll(east, spot, 1)
            from_west = pltpu.roll(west, (lanes - HALO - HALO * (j % PACK)) % lanes, 1)
            around = jnp.where(lane < lanes // 2, from_east, from_west)
            turn = (shift + lanes) & (lanes - 1)
            own = pltpu.roll(reg_ref[t].astype(jnp.float32), turn, 1)
            around = pltpu.roll(around, turn, 1)
            inside = (lane >= shift) & (lane < shift + lanes)
            mid = jnp.where(inside, own, around)
            rest = jnp.where(inside, around, own)
            window = jnp.concatenate([mid, rest], axis=1).astype(jnp.bfloat16)
            low = jnp.dot(row_band_ref[...], window, preferred_element_type=jnp.float32)
            mids.append(mid[RADIUS : RADIUS + rows])
            lows.append(low.astype(jnp.bfloat16))
        low = jnp.dot(
            jnp.concatenate(lows, axis=0), col_band_ref[...], preferred_element_type=jnp.float32
        )
        where = first * rows if isinstance(first, int) else pl.multiple_of(first * rows, rows)
        out_ref[pl.ds(where, count * rows), :] = jnp.concatenate(mids, axis=0) - low

    step = 2 * PACK
    whole = frames // step
    lax.fori_loop(0, whole, lambda g, c: (group(g * step, step), c)[1], 0)
    if frames % step:
        group(whole * step, frames % step)


def project_kernel(first, tile_rows, weight_ref, *refs):
    *parts, keep_ref, pass_ref, send_ref = refs
    count, comps, lanes = keep_ref.shape

    def some(g, carry):
        for j in range(UNROLL):
            i = g * UNROLL + j
            columns = [
                part[pl.ds(first + i, part.shape[0] // tile_rows, stride=tile_rows), :]
                for part in parts
            ]
            picture = jnp.concatenate(columns, axis=0).astype(jnp.bfloat16)
            total = jnp.dot(weight_ref[...], picture, preferred_element_type=jnp.float32)
            total = total.astype(jnp.bfloat16)
            keep_ref[i] = total[:comps]
            pass_ref[i] = total[comps : 2 * comps]
            send_ref[0, i] = total[2 * comps : 3 * comps]
            send_ref[1, i] = total[3 * comps :]
        return carry

    lax.fori_loop(0, count // UNROLL, some, 0)


def tap():
    return jnp.float32(1.0 / (2 * RADIUS + 1))


def row_band(rows):
    shape = (rows, rows + 2 * RADIUS)
    offset = lax.broadcasted_iota(jnp.int32, shape, 1) - lax.broadcasted_iota(jnp.int32, shape, 0)
    return jnp.where((offset >= 0) & (offset <= 2 * RADIUS), tap(), 0.0).astype(jnp.bfloat16)


def col_band(cols, first, width):
    shape = (2 * cols, cols)
    spot = lax.broadcasted_iota(jnp.int32, shape, 0)
    col = jnp.where(spot >= cols + cols // 2, spot - 2 * cols, spot)
    near = jnp.abs(col - lax.broadcasted_iota(jnp.int32, shape, 1)) <= RADIUS
    there = (col + first >= 0) & (col + first < width)
    return jnp.where(near & there, tap(), 0.0).astype(jnp.bfloat16)


def sides_kernel(raw, up, down, out_sem, in_sem):
    rows = raw.shape[1]
    count = lax.axis_size("py")
    me = lax.axis_index("py")
    has_up, has_down = me > 0, me < count - 1
    barrier = pltpu.get_barrier_semaphore()

    for there, step in ((has_up, -1), (has_down, 1)):
        @pl.when(there)
        def _():
            pl.semaphore_signal(
                barrier, inc=1, device_id={"py": me + step}, device_id_type=pl.DeviceIdType.MESH
            )

    both = has_up & has_down

    @pl.when(both)
    def _():
        pl.semaphore_wait(barrier, 2)

    @pl.when(jnp.logical_not(both))
    def _():
        pl.semaphore_wait(barrier, 1)

    moves = []
    for d, (sends, gets, step, first, target) in enumerate(
        ((has_down, has_up, 1, rows - SIDE, up), (has_up, has_down, -1, 0, down))
    ):
        def move(d=d, step=step, first=first, target=target):
            return pltpu.make_async_remote_copy(
                src_ref=raw.at[:, pl.ds(first, SIDE)],
                dst_ref=target,
                send_sem=out_sem.at[d],
                recv_sem=in_sem.at[d],
                device_id={"py": me + step},
                device_id_type=pl.DeviceIdType.MESH,
            )

        moves.append((sends, gets, target, move))

    for sends, gets, target, move in moves:
        @pl.when(sends)
        def _():
            move().start()

    for sends, gets, target, move in moves:
        @pl.when(jnp.logical_not(gets))
        def _():
            target[...] = jnp.zeros_like(target)

    for sends, gets, target, move in moves:
        @pl.when(gets)
        def _():
            move().wait_recv()

    for sends, gets, target, move in moves:
        @pl.when(sends)
        def _():
            move().wait_send()


def sides_of(raw):
    frames, _, cols = raw.shape
    side = jax.ShapeDtypeStruct((frames, SIDE, cols), raw.dtype)
    return pl.pallas_call(
        sides_kernel,
        out_shape=(side, side),
        in_specs=[pl.BlockSpec(memory_space=pl.ANY)],
        out_specs=(VMEM, VMEM),
        scratch_shapes=[pltpu.SemaphoreType.DMA((2,)), pltpu.SemaphoreType.DMA((2,))],
        compiler_params=pltpu.CompilerParams(
            vmem_limit_bytes=24 * 1024 * 1024, collective_id=1, has_side_effects=True
        ),
        name="sides",
    )(raw)


def exchange_kernel(
    to_left, to_right, west, east, hop, second, plain_out, plain_in, out_1, in_1, out_2, in_2, out_3, in_3
):
    count = lax.axis_size("px")
    me = lax.axis_index("px")
    spot, ring = lax.rem(me, RING), lax.div(me, RING)
    rings = count // RING
    packs = to_left.shape[0]
    cuts = [packs * k // 12 for k in range(13)]
    lots = [(0, 1, 2), (3, 4, 5), (6, 7, 8), (9, 10, 11)]

    def piece(ref, k):
        return ref.at[pl.ds(cuts[k], cuts[k + 1] - cuts[k])]

    def kept(ref, d, i, k):
        return ref.at[d, i, pl.ds(0, cuts[k + 1] - cuts[k])]

    def copy(source, target, sent, got, px):
        return pltpu.make_async_remote_copy(
            src_ref=source,
            dst_ref=target,
            send_sem=sent,
            recv_sem=got,
            device_id={"px": px},
            device_id_type=pl.DeviceIdType.MESH,
        )

    barrier = pltpu.get_barrier_semaphore()
    for k in range(1, RING):
        pl.semaphore_signal(
            barrier,
            inc=1,
            device_id={"px": ring * RING + lax.rem(spot + k, RING)},
            device_id_type=pl.DeviceIdType.MESH,
        )
    for step in (1, -1):
        @pl.when((ring + step >= 0) & (ring + step < rings))
        def _():
            pl.semaphore_signal(
                barrier,
                inc=1,
                device_id={"px": me + step * RING},
                device_id_type=pl.DeviceIdType.MESH,
            )
    at_end = (ring == 0) | (ring == rings - 1)

    @pl.when(at_end)
    def _():
        pl.semaphore_wait(barrier, RING)

    @pl.when(jnp.logical_not(at_end))
    def _():
        pl.semaphore_wait(barrier, RING + 1)

    sides = []
    for d, step, source, target, first, final in (
        (0, 1, to_right, west, RING - 1, 0),
        (1, -1, to_left, east, 0, RING - 1),
    ):
        onward = (ring + step >= 0) & (ring + step < rings)
        arriving = (ring - step >= 0) & (ring - step < rings)

        def plain(d=d, step=step, source=source, target=target):
            return copy(source, target, plain_out.at[d], plain_in.at[d], me + step)

        def spread(c, i, k, d=d, source=source):
            return copy(
                piece(source, k), kept(hop, d, i, k), out_1.at[d, c, i], in_1.at[d, i], ring * RING + c
            )

        def cross(c, i, k, d=d, step=step, source=source, target=target, first=first, final=final):
            return copy(
                piece(source, k) if c == first else kept(hop, d, i, k),
                piece(target, k) if c == final else kept(second, d, i, k),
                out_2.at[d, i],
                in_2.at[d, i],
                me + step * RING,
            )

        def gather(c, i, k, d=d, target=target, final=final):
            return copy(
                kept(second, d, i, k),
                piece(target, k),
                out_3.at[d, i],
                in_3.at[d, c, i],
                ring * RING + final,
            )

        sides.append((target, first, final, onward, arriving, plain, spread, cross, gather))

    def each(c):
        return list(enumerate(lots[c]))

    for target, first, final, onward, arriving, plain, spread, cross, gather in sides:
        @pl.when((spot == first) & onward)
        def _():
            for i, k in each(first):
                cross(first, i, k).start()
            for c in range(RING):
                if c != first:
                    for i, k in each(c):
                        spread(c, i, k).start()

    for c in range(RING):
        for i, k in each(c):
            for target, first, final, onward, arriving, plain, spread, cross, gather in sides:
                if c != first:
                    @pl.when((spot == c) & onward)
                    def _():
                        spread(c, i, k).wait_recv()
                        cross(c, i, k).start()

    for target, first, final, onward, arriving, plain, spread, cross, gather in sides:
        @pl.when(spot != first)
        def _():
            plain().start()

    for c in range(RING):
        for i, k in each(c):
            for target, first, final, onward, arriving, plain, spread, cross, gather in sides:
                if c != final:
                    @pl.when((spot == c) & arriving)
                    def _():
                        cross(c, i, k).wait_recv()
                        gather(c, i, k).start()

    for target, first, final, onward, arriving, plain, spread, cross, gather in sides:
        @pl.when((spot == final) & arriving)
        def _():
            for c in range(RING):
                for i, k in each(c):
                    (cross if c == final else gather)(c, i, k).wait_recv()

        @pl.when((spot == final) & jnp.logical_not(arriving))
        def _():
            target[...] = jnp.zeros_like(target)

        @pl.when(spot != final)
        def _():
            plain().wait_recv()

    for target, first, final, onward, arriving, plain, spread, cross, gather in sides:
        @pl.when((spot == first) & onward)
        def _():
            for c in range(RING):
                if c != first:
                    for i, k in each(c):
                        spread(c, i, k).wait_send()

        @pl.when(spot != first)
        def _():
            plain().wait_send()

        for c in range(RING):
            @pl.when((spot == c) & onward)
            def _():
                for i, k in each(c):
                    cross(c, i, k).wait_send()

            if c != final:
                @pl.when((spot == c) & arriving)
                def _():
                    for i, k in each(c):
                        gather(c, i, k).wait_send()


def exchanged(to_left, to_right):
    tile = jax.ShapeDtypeStruct(to_left.shape, to_left.dtype)
    packs = to_left.shape[0]
    kept = pltpu.VMEM((2, 4, -(-packs // 12)) + to_left.shape[1:], to_left.dtype)
    sem = pltpu.SemaphoreType.DMA
    return pl.pallas_call(
        exchange_kernel,
        out_shape=(tile, tile),
        in_specs=[VMEM, VMEM],
        out_specs=(VMEM, VMEM),
        scratch_shapes=[kept, kept, sem((2,)), sem((2,)), sem((2, RING, 4)), sem((2, 4))]
        + [sem((2, 4)), sem((2, 4)), sem((2, 4)), sem((2, RING, 4))],
        compiler_params=pltpu.CompilerParams(
            vmem_limit_bytes=24 * 1024 * 1024, collective_id=0, has_side_effects=True
        ),
        name="exchange",
    )(to_left, to_right)


VMEM = pl.BlockSpec(memory_space=pltpu.VMEM)
SMEM = pl.BlockSpec(memory_space=pltpu.SMEM)
PARAMS = pltpu.CompilerParams(vmem_limit_bytes=40 * 1024 * 1024)


def body(recording, shifts, components):
    frames, rows, cols = recording.shape
    tall = rows + 2 * RADIUS
    part = frames // CHUNKS
    packs = -(-part // PACK)
    py, px = lax.axis_index("py"), lax.axis_index("px")
    height = rows * lax.axis_size("py")
    edge = jnp.stack([RADIUS - py * rows, RADIUS - py * rows + height]).astype(jnp.int32)
    bands = row_band(rows), col_band(cols, px * cols, cols * lax.axis_size("px"))
    filtered = []
    for c in range(CHUNKS):
        raw = recording[c * part : (c + 1) * part]
        shift = shifts[c * part : (c + 1) * part]
        up, down = sides_of(raw)
        tile = jax.ShapeDtypeStruct((packs, tall, cols), jnp.bfloat16)
        reg, to_left, to_right = pl.pallas_call(
            rows_kernel,
            out_shape=(jax.ShapeDtypeStruct((part, tall, cols), jnp.bfloat16), tile, tile),
            in_specs=[SMEM, SMEM, VMEM, VMEM, VMEM],
            out_specs=(VMEM, VMEM, VMEM),
            scratch_shapes=[pltpu.VMEM((PACK, rows + 2 * SIDE, cols), jnp.float32)],
            compiler_params=PARAMS,
            cost_estimate=pl.CostEstimate(flops=10**9, bytes_accessed=10**7, transcendentals=0),
            name="rows",
        )(shift, edge, raw, up, down)
        west, east = exchanged(to_left, to_right)
        filtered.append(
            pl.pallas_call(
                columns_kernel,
                out_shape=jax.ShapeDtypeStruct((part * rows, cols), jnp.float32),
                in_specs=[SMEM] + [VMEM] * 5,
                out_specs=VMEM,
                compiler_params=PARAMS,
                cost_estimate=pl.CostEstimate(flops=10**9, bytes_accessed=10**7, transcendentals=0),
                name="columns",
            )(shift, reg, west, east, *bands)
        )
    groups = lax.axis_size("fr")
    me = lax.axis_index("fr")
    comps = components.shape[1] // groups
    blocks = components.T.reshape(groups, comps, frames)
    weight = jnp.concatenate(
        [lax.dynamic_index_in_dim(blocks, me ^ k, 0, keepdims=False) for k in (0, 2, 1, 3)], axis=0
    )
    count = rows // ROW_CHUNKS
    block = jax.ShapeDtypeStruct((count, comps, cols), jnp.bfloat16)
    pair = jax.ShapeDtypeStruct((2, count, comps, cols), jnp.bfloat16)
    wide = jnp.float32
    done = []
    for c in range(ROW_CHUNKS):
        keep, onward, send = pl.pallas_call(
            functools.partial(project_kernel, c * count, rows),
            out_shape=(block, block, pair),
            in_specs=[VMEM] * (1 + CHUNKS),
            out_specs=(VMEM, VMEM, VMEM),
            compiler_params=PARAMS,
            cost_estimate=pl.CostEstimate(flops=10**9, bytes_accessed=10**7, transcendentals=0),
            name="project",
        )(weight, *filtered)
        near = lax.ppermute(send, "fr", [(i, i ^ 1) for i in range(groups)])
        onward = (onward.astype(wide) + near[1].astype(wide)).astype(jnp.bfloat16)
        far = lax.ppermute(onward, "fr", [(i, i ^ 2) for i in range(groups)])
        total = keep.astype(wide) + near[0].astype(wide) + far.astype(wide)
        done.append(total.astype(jnp.bfloat16))
    return jnp.concatenate(done, axis=0).transpose(1, 0, 2)


def solution(mesh):
    placed = (P("fr", "py", "px"), P("fr", None), P("fr", None))
    return jax.shard_map(
        body, mesh=mesh, in_specs=placed, out_specs=P("fr", "py", "px"), check_vma=False
    )
```
